128 devices in a mesh: row: 16 (over x, y), col: 8 (over z, core).
Axes of the slice: x: 4, y: 4, z: 4, core: 2. Of those that a mesh axis runs over, the one named last changes fastest.
Arguments:
- orbitals: bfloat16 [131072, 512], P(('row', 'col')), may hold values from -6 to 6
- coulomb: bfloat16 [32768, 32768], P('row', 'col'), may hold values from -0.0014648438 to 0.0014648438
- interp: bfloat16 [131072, 1024], P(('row', 'col')), may hold values from -0.1875 to 0.1875
- box_counts: int32 [128], replicated, may hold values from 1 to 768, 32768 in all
- owner_map: int32 [32768], replicated, may hold values from 0 to 32767, as said below
- grid_rows: int32 [128, 1024], P(('row', 'col')), may hold values from 0 to 1023, each once within a row
- listed: int32 [128, 1024], P(('row', 'col')), may hold values from 0 to 255
Outputs:
- exchange_action: float32 [131072, 512], P(('row', 'col'))
The draws below stay inside these ranges and needn't reach their ends.
Inputs may be any that keep to these rules, and one draw needn't show every extreme that they name: `box_counts`: the counts sum to 32768; the largest is exactly 768. `owner_map`: A permutation of the 32768 positions; a point's owner is position // 256. No box holds more than 6 points of one owner, and the box with 768 points holds exactly 6 of some owner. `grid_rows`: each row is a permutation.
All inputs are finite; a program needn't handle non-finite values.
Results may differ from the reference program's by a relative error of at most 0.012.
Values may be sent and summed in bfloat16 or wider, within the bound.
A program may use at most 128 MiB of HBM per device.

```python
import math
import jax
import jax.numpy as jnp
import numpy as np
from jax import lax

NORB = 512
LIST = 1024
OWN = 256
BOX = 1024
BOXES = 128
NMU = 32768
SLOTS = 768
PER = 8
TILE_R = 2048
N_ROW = 16
N_COL = 8


def draw_owner_map(key, part):
    first_key, second_key = jax.random.split(key)
    owner_order = jax.random.permutation(first_key, BOXES)
    local_order = jax.vmap(lambda subkey: jax.random.permutation(subkey, OWN))(jax.random.split(second_key, BOXES))
    listing = jnp.arange(OWN * BOXES)
    owner_ids = owner_order[listing % BOXES]
    local_ids = local_order[owner_ids, listing // BOXES]
    return (owner_ids * OWN + local_ids).astype(jnp.int32)


def plant(array, own_key, low, high):
    shape = array.shape
    spot = [jax.random.randint(jax.random.fold_in(own_key, axis), (), 0, shape[axis]) for axis in range(len(shape))]
    array = array.at[tuple(spot)].set(low)
    longest = shape.index(max(shape))
    spot[longest] = (spot[longest] + 1) % shape[longest]
    return array.at[tuple(spot)].set(high)


def steps_of(rng, dims, cuts, smallest, top_value):
    def one(dim, parts):
        steps = jax.random.uniform(jax.random.fold_in(jax.random.fold_in(rng, 6), dim), (parts,), jnp.float32, smallest / len(cuts), top_value / len(cuts))
        return jnp.repeat(jnp.exp(steps), dims[dim] // parts).reshape((-1,) + (1,) * (len(dims) - dim - 1))

    gain = one(*cuts[0])
    for cut in cuts[1:]:
        gain = gain * one(*cut)
    return gain


def length_profile(amount, total, reach, skew):
    loads = [(1 << 20) // math.isqrt(standing ** skew) + 1 for standing in range(2, amount + 1)]
    surplus, holding = total - reach - (amount - 1), [1] * (amount - 1)
    while surplus > 0:
        free = [i for i in range(amount - 1) if holding[i] < reach]
        mass, budget = sum([loads[i] for i in free]), surplus
        for i in free:
            addition = min(reach - holding[i], max(1, budget * loads[i] // mass), surplus)
            holding[i] = holding[i] + addition
            surplus = surplus - addition
    return np.array([reach] + holding)


def ragged(key, count, total, bound, slope):
    if count == 2:
        one = jax.random.randint(key, (), max(1, total - bound), min(bound, total - 1) + 1)
        return jnp.stack([one, total - one])
    sizes = jnp.asarray(length_profile(count, total, bound, slope), jnp.int32)
    couples = (count - 1) // 2
    donor, sink = sizes[1:1 + 2 * couples:2], sizes[2:2 + 2 * couples:2]
    margin = jnp.minimum(donor - 1, bound - sink)
    moved = jax.random.randint(jax.random.fold_in(key, 1), (couples,), 0, 1 << 20) % (margin + 1)
    sizes = sizes.at[1:1 + 2 * couples:2].set(donor - moved).at[2:2 + 2 * couples:2].set(sink + moved)
    return sizes[jax.random.permutation(jax.random.fold_in(key, 2), count)]


def scatter_about(key, extent, spread, bound, cuts=(), kind=jnp.bfloat16):
    drawn = jax.random.normal(key, extent, jnp.float32) * spread
    if len(cuts) > 0:
        drawn = steps_of(key, extent, cuts, -0.22, 0.18) * drawn
    return jnp.clip(drawn, min=-bound, max=bound).astype(kind)


def setup_inputs(seed: int = 0) -> dict:
    streams_of = jax.random.split(jax.random.key(seed), 8)
    orbitals = scatter_about(streams_of[0], (BOXES * BOX, NORB), 1.0, 6.0, ((0, 128),))
    coulomb = scatter_about(streams_of[1], (NMU, NMU), (NMU * NORB) ** -0.5, 0.0014648438, ((0, 16), (1, 8)))
    interp = scatter_about(streams_of[2], (BOXES * BOX, LIST), LIST ** -0.5, 0.1875, ((0, 128),))
    box_counts = ragged(streams_of[3], BOXES, NMU, SLOTS, 2).astype(jnp.int32)
    owner_map = draw_owner_map(jax.random.fold_in(streams_of[7], 71), 0)
    grid_rows = jax.vmap(lambda own: jax.random.permutation(own, BOX))(jax.random.split(streams_of[5], BOXES)).reshape((BOXES, BOX)).astype(jnp.int32)
    listed = plant(jax.random.randint(streams_of[6], (BOXES, LIST), 0, OWN), jax.random.fold_in(streams_of[6], 1), 0, OWN - 1).astype(jnp.int32)
    return {"orbitals": orbitals, "coulomb": coulomb, "interp": interp, "box_counts": box_counts, "owner_map": owner_map, "grid_rows": grid_rows, "listed": listed}


def reference(orbitals, coulomb, interp, box_counts, owner_map, grid_rows, listed):
    box_total = N_ROW * N_COL
    point_total = OWN * box_total
    box_ends = jnp.cumsum(box_counts).astype(jnp.int32)
    starts = (box_ends - box_counts).astype(jnp.int32)
    listing = jnp.arange(point_total, dtype=jnp.int32)
    source = jnp.sum((listing[:, None] >= box_ends[None, :]).astype(jnp.int32), axis=1).astype(jnp.int32)
    within = (listing - starts[source]).astype(jnp.int32)
    grid_index = (source * BOX + grid_rows[source, within]).astype(jnp.int32)
    point_rows = jnp.zeros((point_total, NORB), jnp.bfloat16).at[owner_map].set(orbitals[grid_index])
    column_rows = point_rows.reshape(N_ROW, N_COL, OWN, NORB).transpose(1, 0, 2, 3).reshape(point_total, NORB)
    right_rows = column_rows.astype(jnp.float32)

    def row_block(pieces):
        left_rows, kernel_rows = pieces
        pair_tile = jnp.dot(left_rows.astype(jnp.float32), right_rows.T, precision=lax.Precision.HIGHEST).astype(jnp.bfloat16)
        weighted = (pair_tile.astype(jnp.float32) * kernel_rows.astype(jnp.float32)).astype(jnp.bfloat16)
        return jnp.dot(weighted.astype(jnp.float32), right_rows, precision=lax.Precision.HIGHEST)

    projected = lax.map(row_block, (point_rows.reshape(N_ROW, TILE_R, NORB), coulomb.reshape(N_ROW, TILE_R, point_total)))
    projected = projected.reshape(point_total, NORB).astype(jnp.bfloat16)
    positions = ((jnp.arange(LIST, dtype=jnp.int32) // PER)[None, :] * OWN + listed).astype(jnp.int32)
    selected = projected[positions]

    def one_box(pieces):
        coeffs, chosen = pieces
        return -jnp.dot(coeffs.astype(jnp.float32), chosen.astype(jnp.float32), precision=lax.Precision.HIGHEST)

    result = lax.map(one_box, (interp.reshape(box_total, BOX, LIST), selected))
    return result.reshape(box_total * BOX, NORB)
```

```python
import jax
import jax.numpy as jnp
from jax import lax
from jax.sharding import PartitionSpec as P

NORB = 512
LIST = 1024
OWN = 256
SLOTS = 768
BOTH = ("row", "col")
F32 = jnp.float32
BF16 = jnp.bfloat16


def exchange(chunks):
    return lax.all_to_all(chunks, BOTH, split_axis=0, concat_axis=0, tiled=True)


def pick(index, rows, count):
    one_hot = (index[:, None] == jnp.arange(count, dtype=jnp.int32)[None, :]).astype(BF16)
    return jnp.dot(one_hot, rows, preferred_element_type=F32).astype(BF16)


def add_block(shard_rows, left_rows, kernel_tile):
    pair_tile = jnp.einsum(
        "ak,bk->ab", left_rows, shard_rows, preferred_element_type=F32
    ).astype(BF16)
    weighted = (pair_tile.astype(F32) * kernel_tile.astype(F32)).astype(BF16)
    return jnp.dot(weighted, shard_rows, preferred_element_type=F32)


def outgoing_chunks(orbitals, box_counts, owner_map, grid_rows, listed, my_box, box_total, lanes):
    per_owner = LIST // box_total
    box_ids = jnp.arange(box_total, dtype=jnp.int32)
    first_point = jnp.sum(jnp.where(box_ids < my_box, box_counts, 0))
    my_count = jnp.sum(jnp.where(box_ids == my_box, box_counts, 0))
    slot_ids = jnp.arange(SLOTS, dtype=jnp.int32)
    is_live = slot_ids < my_count
    padded = jnp.concatenate([owner_map, jnp.zeros((SLOTS,), jnp.int32)])
    position = lax.dynamic_slice(padded, (first_point,), (SLOTS,))
    owner_ids = position // OWN
    local_ids = position - owner_ids * OWN
    matches = (
        (owner_ids[:, None] == owner_ids[None, :])
        & is_live[None, :]
        & (slot_ids[None, :] < slot_ids[:, None])
    )
    pair_rank = jnp.sum(matches.astype(jnp.int32), axis=1)
    target = jnp.where(is_live, owner_ids * lanes + pair_rank, -1)
    dest = jnp.arange(box_total * lanes, dtype=jnp.int32)
    hits = target[None, :] == dest[:, None]
    coded = (grid_rows[0, :SLOTS] + 1) * OWN + local_ids
    found = jnp.sum(jnp.where(hits, coded[None, :], 0), axis=1)
    grid = found // OWN - 1
    local = jnp.where(found > 0, found - (grid + 1) * OWN, -1)
    picked = pick(grid, orbitals, orbitals.shape[0]).reshape(box_total, lanes, NORB)
    meta = jnp.stack([listed[0].reshape(box_total, per_owner), local.reshape(box_total, lanes)], axis=1)
    meta = jnp.pad(meta.astype(BF16), ((0, 0), (lanes - 2, 0), (0, NORB - per_owner)))
    row_ids = jnp.arange(lanes)[None, :, None]
    return jnp.where(row_ids < lanes - 2, picked, meta)


def shards(orbitals, coulomb, interp, box_counts, owner_map, grid_rows, listed):
    box_total = lax.axis_size("row") * lax.axis_size("col")
    lanes = LIST // box_total
    my_box = lax.axis_index("row") * lax.axis_size("col") + lax.axis_index("col")
    received = exchange(
        outgoing_chunks(orbitals, box_counts, owner_map, grid_rows, listed, my_box, box_total, lanes)
    )
    wanted = received[:, lanes - 2, :lanes].astype(jnp.int32).reshape(-1)
    local = received[:, lanes - 1, :lanes].astype(jnp.int32).reshape(-1)
    place = (local[None, :] == jnp.arange(OWN, dtype=jnp.int32)[:, None]).astype(BF16)
    owned_rows = jnp.dot(
        place, received.reshape(box_total * lanes, NORB), preferred_element_type=F32
    ).astype(BF16)
    left_rows = lax.all_gather(owned_rows, "col", axis=0, tiled=True)
    column_rows = lax.all_gather(owned_rows, "row", axis=0, tiled=True)
    partial_sums = add_block(column_rows, left_rows, coulomb)
    owned_result = lax.psum_scatter(partial_sums, "col", scatter_dimension=0, tiled=True).astype(BF16)
    fetched = exchange(pick(wanted, owned_result, OWN).reshape(box_total, lanes, NORB))
    return -jnp.dot(interp, fetched.reshape(LIST, NORB), preferred_element_type=F32)


def solution(mesh):
    return jax.shard_map(
        shards,
        mesh=mesh,
        in_specs=(
            P(BOTH, None),
            P("row", "col"),
            P(BOTH, None),
            P(),
            P(),
            P(BOTH, None),
            P(BOTH, None),
        ),
        out_specs=P(BOTH, None),
        check_vma=False,
    )
```

```python
import jax
import jax.numpy as jnp
from jax import lax
from jax.experimental import pallas as pl
from jax.experimental.pallas import tpu as pltpu
from jax.sharding import PartitionSpec as P

NORB = 512
LIST = 1024
OWN = 256
SLOTS = 768
BOTH = ("row", "col")
F32 = jnp.float32
BF16 = jnp.bfloat16


SIDE = 4
MESH = pl.DeviceIdType.MESH


def greet(partners):
    barrier = pltpu.get_barrier_semaphore()
    for partner in partners:
        pl.semaphore_signal(barrier, inc=1, device_id=partner, device_id_type=MESH)
    pl.semaphore_wait(barrier, len(partners))


def exchange_kernel(rows, cols, src, dst, send_sem, recv_sem, own_sem):
    me = lax.axis_index("row") * cols + lax.axis_index("col")
    count = rows * cols
    barrier = pltpu.get_barrier_semaphore()

    def place(step):
        other = lax.rem(me + step, count)
        return other, (other // cols, lax.rem(other, cols))

    def signal(step, carry):
        pl.semaphore_signal(barrier, inc=1, device_id=place(step)[1], device_id_type=MESH)
        return carry

    lax.fori_loop(1, count, signal, 0)
    own = pltpu.make_async_copy(src.at[me], dst.at[me], own_sem)
    own.start()
    pl.semaphore_wait(barrier, count - 1)

    def send(step, carry):
        other, device = place(step)
        pltpu.make_async_remote_copy(
            src_ref=src.at[other],
            dst_ref=dst.at[me],
            send_sem=send_sem,
            recv_sem=recv_sem,
            device_id=device,
            device_id_type=MESH,
        ).start()
        return carry

    lax.fori_loop(1, count, send, 0)
    own.wait()
    many = pl.ds(0, count - 1)
    pltpu.make_async_copy(src.at[many], dst.at[many], send_sem).wait()
    pltpu.make_async_copy(src.at[many], dst.at[many], recv_sem).wait()


def exchange(chunks, collective_id):
    return pl.pallas_call(
        lambda *refs: exchange_kernel(lax.axis_size("row"), lax.axis_size("col"), *refs),
        out_shape=jax.ShapeDtypeStruct(chunks.shape, chunks.dtype),
        in_specs=[pl.BlockSpec(memory_space=pltpu.VMEM)],
        out_specs=pl.BlockSpec(memory_space=pltpu.VMEM),
        scratch_shapes=[pltpu.SemaphoreType.DMA] * 3,
        compiler_params=pltpu.CompilerParams(collective_id=collective_id, has_side_effects=True),
    )(chunks)


def around(at):
    return lax.rem(at + SIDE - 1, SIDE), lax.rem(at + 1, SIDE), lax.rem(at + 2, SIDE)


def gather_kernel(own, buf, left, send_sem, recv_sem, own_sem):
    row, col = lax.axis_index("row"), lax.axis_index("col")
    x, y = row // SIDE, lax.rem(row, SIDE)
    z, core = col // 2, lax.rem(col, 2)
    (xm, xp, xf), (ym, yp, yf), (zm, zp, zf) = around(x), around(y), around(z)
    on_x = ((xm * SIDE + y, col), (xp * SIDE + y, col))
    on_y = ((x * SIDE + ym, col), (x * SIDE + yp, col))
    on_z = ((row, zm * 2 + core), (row, zp * 2 + core))
    mate = (row, z * 2 + 1 - core)
    used, started = [0], []

    def push(src, dst, device, landing):
        index = used[0]
        used[0] += 1
        pair = send_sem.at[index], recv_sem.at[index]
        copy = pltpu.make_async_remote_copy(src, dst, *pair, device_id=device, device_id_type=MESH)
        copy.start()
        started.append(copy)
        return pltpu.make_async_remote_copy(landing, landing, *pair, device_id=device, device_id_type=MESH)

    greet([*on_x, *on_y, *on_z, mate])
    local = [
        pltpu.make_async_copy(own, buf.at[x, y], own_sem.at[0]),
        pltpu.make_async_copy(own, left.at[z, core], own_sem.at[1]),
    ]
    for copy in local:
        copy.start()

    def slot(half, first, second):
        return buf.at[second, first, 0] if half == 0 else buf.at[first, second, 1]

    first_at = ((ym, y, yp, yf), (xm, x, xp, xf))
    second_at = ((xm, x, xp, xf), (ym, y, yp, yf))
    first_to, second_to = (on_y, on_x), (on_x, on_y)

    def second_send(half, first, src=None):
        minus, at, plus, _ = second_at[half]
        here = slot(half, first, at)
        src = here if src is None else src
        return (
            push(src, here, second_to[half][1], slot(half, first, minus)),
            push(src, here, second_to[half][0], slot(half, first, plus)),
        )

    def relay(ring, targets, where):
        minus, _, plus, far = ring
        one = push(where(minus).at[0], where(minus).at[0], targets[1], where(far).at[0])
        two = push(where(plus).at[1], where(plus).at[1], targets[0], where(far).at[1])
        return one, two

    first_waits = []
    for half in range(2):
        minus, at, plus, _ = first_at[half]
        here = slot(half, at, second_at[half][1])
        first_waits.append((
            push(own.at[half], here, first_to[half][1], slot(half, minus, second_at[half][1])),
            push(own.at[half], here, first_to[half][0], slot(half, plus, second_at[half][1])),
        ))
    second_waits = [[(first_at[h][1], second_send(h, first_at[h][1], own.at[h]))] for h in range(2)]
    z_waits = (
        push(own, left.at[z, core], on_z[1], left.at[zm, core]),
        push(own, left.at[z, core], on_z[0], left.at[zp, core]),
    )
    mate_waits = [push(own, left.at[z, core], mate, left.at[z, 1 - core])]
    first_far = []
    for half in range(2):
        for wait in first_waits[half]:
            wait.wait_recv()
        at = second_at[half][1]
        first_far.append(relay(first_at[half], first_to[half], lambda f, h=half, s=at: slot(h, f, s)))
        for k in (0, 2):
            second_waits[half].append((first_at[half][k], second_send(half, first_at[half][k])))
    for wait in z_waits:
        wait.wait_recv()
    z_far = relay((zm, z, zp, zf), on_z, lambda at: left.at[at, core])
    for at in (zm, zp):
        mate_waits.append(push(left.at[at, core], left.at[at, core], mate, left.at[at, 1 - core]))
    last = []

    def second_relay(half, first, waits):
        for wait in waits:
            wait.wait_recv()
        last.extend(relay(second_at[half], second_to[half], lambda s: slot(half, first, s)))

    for half in range(2):
        second_relay(half, *second_waits[half][0])
    for half in range(2):
        for wait in first_far[half]:
            wait.wait_recv()
        far = first_at[half][3]
        second_waits[half].append((far, second_send(half, far)))
    for wait in z_far:
        wait.wait_recv()
    mate_waits.append(push(left.at[zf, core], left.at[zf, core], mate, left.at[zf, 1 - core]))
    for k in (1, 2, 3):
        for half in range(2):
            second_relay(half, *second_waits[half][k])
    for wait in last + mate_waits:
        wait.wait_recv()
    for copy in started:
        copy.wait_send()
    for copy in local:
        copy.wait()


COPIES = 2 * (4 + 4 * 4) + 4 + 4


def gather_rows(owned_rows):
    rows, norb = owned_rows.shape
    own = owned_rows.reshape(2, 2, rows // 4, norb)
    vmem = pl.BlockSpec(memory_space=pltpu.VMEM)
    buf, left = pl.pallas_call(
        gather_kernel,
        out_shape=(
            jax.ShapeDtypeStruct((SIDE, SIDE, *own.shape), own.dtype),
            jax.ShapeDtypeStruct((SIDE, 2, *own.shape), own.dtype),
        ),
        in_specs=[vmem],
        out_specs=(vmem, vmem),
        scratch_shapes=[
            pltpu.SemaphoreType.DMA((COPIES,)),
            pltpu.SemaphoreType.DMA((COPIES,)),
            pltpu.SemaphoreType.DMA((2,)),
        ],
        compiler_params=pltpu.CompilerParams(collective_id=1, has_side_effects=True),
    )(own)
    return buf.reshape(-1, norb), left.reshape(-1, norb)


STRIP = 32


def scatter_kernel(src, out, inbox, stage, halves, blocks, send_sem, recv_sem):
    row, col = lax.axis_index("row"), lax.axis_index("col")
    z, core = col // 2, lax.rem(col, 2)
    zm, zp, zf = around(z)
    minus, plus = (row, zm * 2 + core), (row, zp * 2 + core)
    mate = (row, z * 2 + 1 - core)
    half = src.shape[2] // 2
    greet([minus, plus, mate])

    def push(index, src_ref, dst_ref, device):
        copy = pltpu.make_async_remote_copy(
            src_ref, dst_ref, send_sem.at[index], recv_sem.at[index], device_id=device, device_id_type=MESH
        )
        copy.start()
        return copy

    mates = [push(i, src.at[at, 1 - core], inbox.at[at], mate) for i, at in enumerate((zf, zp, zm, z))]

    def add(at, start, size, write, *more):
        @pl.loop(0, size // STRIP)
        def _(i):
            rows = pl.ds(pl.multiple_of(start + i * STRIP, STRIP), STRIP)
            total = src[at, core, rows, :].astype(F32) + inbox[at, rows, :].astype(F32)
            for ref, shift in more:
                part = pl.ds(pl.multiple_of(start - shift + i * STRIP, STRIP), STRIP)
                total += ref[part, :].astype(F32)
            write[rows, :] = total.astype(BF16)

    mates[0].wait_recv()
    add(zf, 0, 2 * half, stage.at[0])
    up = push(4, stage.at[0, pl.ds(0, half)], halves.at[0], plus)
    down = push(5, stage.at[0, pl.ds(half, half)], halves.at[1], minus)
    mates[1].wait_recv()
    add(zp, half, half, stage.at[1])
    mates[2].wait_recv()
    add(zm, 0, half, stage.at[2])
    up.wait_recv()
    add(zp, 0, half, stage.at[1], (halves.at[0], 0))
    up_block = push(6, stage.at[1], blocks.at[0], plus)
    down.wait_recv()
    add(zm, half, half, stage.at[2], (halves.at[1], half))
    down_block = push(7, stage.at[2], blocks.at[1], minus)
    mates[3].wait_recv()
    up_block.wait_recv()
    down_block.wait_recv()
    add(z, 0, 2 * half, out, (blocks.at[0], 0), (blocks.at[1], 0))
    for copy in (*mates, up, down, up_block, down_block):
        copy.wait_send()


def scatter_sums(partial_sums):
    norb = partial_sums.shape[1]
    vmem = pl.BlockSpec(memory_space=pltpu.VMEM)
    return pl.pallas_call(
        scatter_kernel,
        out_shape=jax.ShapeDtypeStruct((OWN, norb), BF16),
        in_specs=[vmem],
        out_specs=vmem,
        scratch_shapes=[
            pltpu.VMEM((SIDE, OWN, norb), BF16),
            pltpu.VMEM((3, OWN, norb), BF16),
            pltpu.VMEM((2, OWN // 2, norb), BF16),
            pltpu.VMEM((2, OWN, norb), BF16),
            pltpu.SemaphoreType.DMA((8,)),
            pltpu.SemaphoreType.DMA((8,)),
        ],
        compiler_params=pltpu.CompilerParams(collective_id=2, has_side_effects=True),
    )(partial_sums.reshape(SIDE, 2, OWN, norb))


def pick(index, rows, count):
    one_hot = (index[:, None] == jnp.arange(count, dtype=jnp.int32)[None, :]).astype(BF16)
    return jnp.dot(one_hot, rows, preferred_element_type=F32).astype(BF16)


def add_block(shard_rows, left_rows, kernel_tile):
    pair_tile = jnp.einsum(
        "ak,bk->ab", left_rows, shard_rows, preferred_element_type=F32
    ).astype(BF16)
    weighted = (pair_tile.astype(F32) * kernel_tile.astype(F32)).astype(BF16)
    return jnp.dot(weighted, shard_rows, preferred_element_type=F32)


def outgoing_chunks(orbitals, box_counts, owner_map, grid_rows, listed, my_box, box_total, lanes):
    per_owner = LIST // box_total
    box_ids = jnp.arange(box_total, dtype=jnp.int32)
    first_point = jnp.sum(jnp.where(box_ids < my_box, box_counts, 0))
    my_count = jnp.sum(jnp.where(box_ids == my_box, box_counts, 0))
    slot_ids = jnp.arange(SLOTS, dtype=jnp.int32)
    is_live = slot_ids < my_count
    padded = jnp.concatenate([owner_map, jnp.zeros((SLOTS,), jnp.int32)])
    position = lax.dynamic_slice(padded, (first_point,), (SLOTS,))
    owner_ids = position // OWN
    local_ids = position - owner_ids * OWN
    matches = (
        (owner_ids[:, None] == owner_ids[None, :])
        & is_live[None, :]
        & (slot_ids[None, :] < slot_ids[:, None])
    )
    pair_rank = jnp.sum(matches.astype(jnp.int32), axis=1)
    target = jnp.where(is_live, owner_ids * lanes + pair_rank, -1)
    dest = jnp.arange(box_total * lanes, dtype=jnp.int32)
    hits = target[None, :] == dest[:, None]
    coded = (grid_rows[0, :SLOTS] + 1) * OWN + local_ids
    found = jnp.sum(jnp.where(hits, coded[None, :], 0), axis=1)
    grid = found // OWN - 1
    local = jnp.where(found > 0, found - (grid + 1) * OWN, -1)
    picked = pick(grid, orbitals, orbitals.shape[0]).reshape(box_total, lanes, NORB)
    meta = jnp.stack([listed[0].reshape(box_total, per_owner), local.reshape(box_total, lanes)], axis=1)
    meta = jnp.pad(meta.astype(BF16), ((0, 0), (lanes - 2, 0), (0, NORB - per_owner)))
    row_ids = jnp.arange(lanes)[None, :, None]
    return jnp.where(row_ids < lanes - 2, picked, meta)


def shards(orbitals, coulomb, interp, box_counts, owner_map, grid_rows, listed):
    box_total = lax.axis_size("row") * lax.axis_size("col")
    lanes = LIST // box_total
    my_box = lax.axis_index("row") * lax.axis_size("col") + lax.axis_index("col")
    received = exchange(
        outgoing_chunks(orbitals, box_counts, owner_map, grid_rows, listed, my_box, box_total, lanes),
        0,
    )
    wanted = received[:, lanes - 2, :lanes].astype(jnp.int32).reshape(-1)
    local = received[:, lanes - 1, :lanes].astype(jnp.int32).reshape(-1)
    place = (local[None, :] == jnp.arange(OWN, dtype=jnp.int32)[:, None]).astype(BF16)
    owned_rows = jnp.dot(
        place, received.reshape(box_total * lanes, NORB), preferred_element_type=F32
    ).astype(BF16)
    column_rows, left_rows = gather_rows(owned_rows)
    partial_sums = add_block(column_rows, left_rows, coulomb).astype(BF16)
    owned_result = scatter_sums(partial_sums)
    fetched = exchange(pick(wanted, owned_result, OWN).reshape(box_total, lanes, NORB), 3)
    return -jnp.dot(interp, fetched.reshape(LIST, NORB), preferred_element_type=F32)


def solution(mesh):
    return jax.shard_map(
        shards,
        mesh=mesh,
        in_specs=(
            P(BOTH, None),
            P("row", "col"),
            P(BOTH, None),
            P(),
            P(),
            P(BOTH, None),
            P(BOTH, None),
        ),
        out_specs=P(BOTH, None),
        check_vma=False,
    )
```

```python
import jax
import jax.numpy as jnp
from jax import lax
from jax.experimental import pallas as pl
from jax.experimental.pallas import tpu as pltpu
from jax.sharding import PartitionSpec as P

NORB = 512
LIST = 1024
OWN = 256
SLOTS = 768
BOTH = ("row", "col")
F32 = jnp.float32
BF16 = jnp.bfloat16


SIDE = 4
MESH = pl.DeviceIdType.MESH


def greet(partners):
    barrier = pltpu.get_barrier_semaphore()
    for partner in partners:
        pl.semaphore_signal(barrier, inc=1, device_id=partner, device_id_type=MESH)
    pl.semaphore_wait(barrier, len(partners))


def exchange_kernel(rows, cols, src, dst, send_sem, recv_sem, own_sem):
    me = lax.axis_index("row") * cols + lax.axis_index("col")
    count = rows * cols
    barrier = pltpu.get_barrier_semaphore()

    def place(step):
        other = lax.rem(me + step, count)
        return other, (other // cols, lax.rem(other, cols))

    def signal(step, carry):
        pl.semaphore_signal(barrier, inc=1, device_id=place(step)[1], device_id_type=MESH)
        return carry

    lax.fori_loop(1, count, signal, 0)
    own = pltpu.make_async_copy(src.at[me], dst.at[me], own_sem)
    own.start()
    pl.semaphore_wait(barrier, count - 1)

    def send(step, carry):
        other, device = place(step)
        pltpu.make_async_remote_copy(
            src_ref=src.at[other],
            dst_ref=dst.at[me],
            send_sem=send_sem,
            recv_sem=recv_sem,
            device_id=device,
            device_id_type=MESH,
        ).start()
        return carry

    lax.fori_loop(1, count, send, 0)
    own.wait()
    many = pl.ds(0, count - 1)
    pltpu.make_async_copy(src.at[many], dst.at[many], send_sem).wait()
    pltpu.make_async_copy(src.at[many], dst.at[many], recv_sem).wait()


def exchange(chunks, collective_id):
    return pl.pallas_call(
        lambda *refs: exchange_kernel(lax.axis_size("row"), lax.axis_size("col"), *refs),
        out_shape=jax.ShapeDtypeStruct(chunks.shape, chunks.dtype),
        in_specs=[pl.BlockSpec(memory_space=pltpu.VMEM)],
        out_specs=pl.BlockSpec(memory_space=pltpu.VMEM),
        scratch_shapes=[pltpu.SemaphoreType.DMA] * 3,
        compiler_params=pltpu.CompilerParams(collective_id=collective_id, has_side_effects=True),
    )(chunks)


def around(at):
    return lax.rem(at + SIDE - 1, SIDE), lax.rem(at + 1, SIDE), lax.rem(at + 2, SIDE)


def project_kernel(own, coulomb, out, buf, left, tile, acc, send_sem, recv_sem, own_sem):
    row, col = lax.axis_index("row"), lax.axis_index("col")
    x, y = row // SIDE, lax.rem(row, SIDE)
    z, core = col // 2, lax.rem(col, 2)
    (xm, xp, xf), (ym, yp, yf), (zm, zp, zf) = around(x), around(y), around(z)
    on_x = ((xm * SIDE + y, col), (xp * SIDE + y, col))
    on_y = ((x * SIDE + ym, col), (x * SIDE + yp, col))
    on_z = ((row, zm * 2 + core), (row, zp * 2 + core))
    mate = (row, z * 2 + 1 - core)
    used, started = [0], []
    tile_in = pltpu.make_async_copy(coulomb, tile, own_sem.at[2])
    tile_in.start()

    def push(src, dst, device, landing):
        index = used[0]
        used[0] += 1
        pair = send_sem.at[index], recv_sem.at[index]
        copy = pltpu.make_async_remote_copy(src, dst, *pair, device_id=device, device_id_type=MESH)
        copy.start()
        started.append(copy)
        return pltpu.make_async_remote_copy(landing, landing, *pair, device_id=device, device_id_type=MESH)

    def left_of(at_z, at_core):
        return left.at[at_z * 2 + at_core]

    greet([*on_x, *on_y, *on_z, mate])
    local = [pltpu.make_async_copy(own, buf.at[x, y], own_sem.at[0])]
    local += [
        pltpu.make_async_copy(own.at[:, q], left_of(z, core).at[:, pl.ds(64 * q, 64)], own_sem.at[1 + 2 * q])
        for q in range(2)
    ]
    for copy in local:
        copy.start()

    def slot(half, first, second):
        return buf.at[second, first, 0] if half == 0 else buf.at[first, second, 1]

    first_at = ((ym, y, yp, yf), (xm, x, xp, xf))
    second_at = ((xm, x, xp, xf), (ym, y, yp, yf))
    first_to, second_to = (on_y, on_x), (on_x, on_y)

    def second_send(half, first, src=None):
        minus, at, plus, _ = second_at[half]
        here = slot(half, first, at)
        src = here if src is None else src
        return (
            push(src, here, second_to[half][1], slot(half, first, minus)),
            push(src, here, second_to[half][0], slot(half, first, plus)),
        )

    def relay(ring, targets, where):
        minus, _, plus, far = ring
        one = push(where(minus).at[0], where(minus).at[0], targets[1], where(far).at[0])
        two = push(where(plus).at[1], where(plus).at[1], targets[0], where(far).at[1])
        return one, two

    first_waits = []
    for half in range(2):
        minus, at, plus, _ = first_at[half]
        here = slot(half, at, second_at[half][1])
        first_waits.append((
            push(own.at[half], here, first_to[half][1], slot(half, minus, second_at[half][1])),
            push(own.at[half], here, first_to[half][0], slot(half, plus, second_at[half][1])),
        ))
    second_waits = [[(first_at[h][1], second_send(h, first_at[h][1], own.at[h]))] for h in range(2)]
    for copy in local:
        copy.wait()
    mine = left_of(z, core)
    z_waits = (
        push(mine, mine, on_z[1], left_of(zm, core)),
        push(mine, mine, on_z[0], left_of(zp, core)),
    )
    mate_waits = [push(mine, mine, mate, left_of(z, 1 - core))]
    first_far = []
    for half in range(2):
        for wait in first_waits[half]:
            wait.wait_recv()
        at = second_at[half][1]
        first_far.append(relay(first_at[half], first_to[half], lambda f, h=half, s=at: slot(h, f, s)))
        for k in (0, 2):
            second_waits[half].append((first_at[half][k], second_send(half, first_at[half][k])))
    for wait in z_waits:
        wait.wait_recv()
    z_far = relay((zm, z, zp, zf), on_z, lambda at: left_of(at, core))
    for at in (zm, zp):
        mate_waits.append(push(left_of(at, core), left_of(at, core), mate, left_of(at, 1 - core)))
    relayed = {}

    def second_relay(half, k):
        first, waits = second_waits[half][k]
        for wait in waits:
            wait.wait_recv()
        relayed[half, k] = relay(second_at[half], second_to[half], lambda s: slot(half, first, s))

    def landed(*keys):
        for key in keys:
            for wait in relayed.pop(key):
                wait.wait_recv()

    first_step = [True]

    def project(one, two, final=False):
        start = first_step[0]
        first_step[0] = False

        @pl.loop(0, left.shape[0])
        def _(m):
            left_rows = left[m].reshape(OWN, -1)
            total = None
            for bx, by in (one, two):
                rows = buf[bx, by].reshape(OWN, -1)
                pair = lax.dot_general(
                    left_rows, rows, (((1,), (1,)), ((), ())), preferred_element_type=F32
                ).astype(BF16)
                at = pl.multiple_of((bx * SIDE + by) * OWN, OWN)
                weights = tile[pl.ds(pl.multiple_of(m * OWN, OWN), OWN), pl.ds(at, OWN)]
                part = jnp.dot(pair * weights, rows, preferred_element_type=F32)
                total = part if total is None else total + part
            if not start:
                total = acc[m] + total
            if final:
                out[m] = total.astype(BF16)
            else:
                acc[m] = total

    for half in range(2):
        second_relay(half, 0)
    for half in range(2):
        for wait in first_far[half]:
            wait.wait_recv()
        far = first_at[half][3]
        second_waits[half].append((far, second_send(half, far)))
    for wait in z_far:
        wait.wait_recv()
    mate_waits.append(push(left_of(zf, core), left_of(zf, core), mate, left_of(zf, 1 - core)))
    for wait in mate_waits:
        wait.wait_recv()
    tile_in.wait()
    project((x, y), (x, ym))
    second_relay(0, 1)
    second_relay(1, 1)
    project((x, yp), (xm, y))
    second_relay(0, 2)
    second_relay(1, 2)
    project((xp, y), (xm, ym))
    second_relay(0, 3)
    second_relay(1, 3)
    project((xm, yp), (xp, ym))
    landed((0, 0), (1, 0))
    project((xp, yp), (x, yf))
    landed((1, 1), (1, 2), (0, 1), (0, 2))
    project((xf, y), (xm, yf))
    project((xp, yf), (xf, ym))
    landed((0, 3), (1, 3))
    project((xf, yp), (xf, yf), True)
    for copy in started:
        copy.wait_send()


COPIES = 2 * (4 + 4 * 4) + 4 + 4


def project_rows(owned_rows, coulomb):
    rows, norb = owned_rows.shape
    own = owned_rows.reshape(2, 2, rows // 4, norb)
    cols = coulomb.shape[0] // rows
    vmem = pl.BlockSpec(memory_space=pltpu.VMEM)
    return pl.pallas_call(
        project_kernel,
        out_shape=jax.ShapeDtypeStruct((cols, rows, norb), BF16),
        in_specs=[vmem, pl.BlockSpec(memory_space=pl.ANY)],
        out_specs=vmem,
        scratch_shapes=[
            pltpu.VMEM((SIDE, SIDE, *own.shape), BF16),
            pltpu.VMEM((cols, 2, rows // 2, norb), BF16),
            pltpu.VMEM(coulomb.shape, BF16),
            pltpu.VMEM((cols, rows, norb), F32),
            pltpu.SemaphoreType.DMA((COPIES,)),
            pltpu.SemaphoreType.DMA((COPIES,)),
            pltpu.SemaphoreType.DMA((4,)),
        ],
        compiler_params=pltpu.CompilerParams(
            collective_id=1, has_side_effects=True, vmem_limit_bytes=48 * 1024 * 1024
        ),
    )(own, coulomb)


STRIP = 32


def scatter_kernel(src, out, inbox, stage, halves, blocks, send_sem, recv_sem):
    row, col = lax.axis_index("row"), lax.axis_index("col")
    z, core = col // 2, lax.rem(col, 2)
    zm, zp, zf = around(z)
    minus, plus = (row, zm * 2 + core), (row, zp * 2 + core)
    mate = (row, z * 2 + 1 - core)
    half = src.shape[2] // 2
    greet([minus, plus, mate])

    def push(index, src_ref, dst_ref, device):
        copy = pltpu.make_async_remote_copy(
            src_ref, dst_ref, send_sem.at[index], recv_sem.at[index], device_id=device, device_id_type=MESH
        )
        copy.start()
        return copy

    mates = [push(i, src.at[at, 1 - core], inbox.at[at], mate) for i, at in enumerate((zf, zp, zm, z))]

    def add(at, start, size, write, *more):
        @pl.loop(0, size // STRIP)
        def _(i):
            rows = pl.ds(pl.multiple_of(start + i * STRIP, STRIP), STRIP)
            total = src[at, core, rows, :].astype(F32) + inbox[at, rows, :].astype(F32)
            for ref, shift in more:
                part = pl.ds(pl.multiple_of(start - shift + i * STRIP, STRIP), STRIP)
                total += ref[part, :].astype(F32)
            write[rows, :] = total.astype(BF16)

    mates[0].wait_recv()
    add(zf, 0, 2 * half, stage.at[0])
    up = push(4, stage.at[0, pl.ds(0, half)], halves.at[0], plus)
    down = push(5, stage.at[0, pl.ds(half, half)], halves.at[1], minus)
    mates[1].wait_recv()
    add(zp, half, half, stage.at[1])
    mates[2].wait_recv()
    add(zm, 0, half, stage.at[2])
    up.wait_recv()
    add(zp, 0, half, stage.at[1], (halves.at[0], 0))
    up_block = push(6, stage.at[1], blocks.at[0], plus)
    down.wait_recv()
    add(zm, half, half, stage.at[2], (halves.at[1], half))
    down_block = push(7, stage.at[2], blocks.at[1], minus)
    mates[3].wait_recv()
    up_block.wait_recv()
    down_block.wait_recv()
    add(z, 0, 2 * half, out, (blocks.at[0], 0), (blocks.at[1], 0))
    for copy in (*mates, up, down, up_block, down_block):
        copy.wait_send()


def scatter_sums(partial_sums):
    norb = partial_sums.shape[-1]
    vmem = pl.BlockSpec(memory_space=pltpu.VMEM)
    return pl.pallas_call(
        scatter_kernel,
        out_shape=jax.ShapeDtypeStruct((OWN, norb), BF16),
        in_specs=[vmem],
        out_specs=vmem,
        scratch_shapes=[
            pltpu.VMEM((SIDE, OWN, norb), BF16),
            pltpu.VMEM((3, OWN, norb), BF16),
            pltpu.VMEM((2, OWN // 2, norb), BF16),
            pltpu.VMEM((2, OWN, norb), BF16),
            pltpu.SemaphoreType.DMA((8,)),
            pltpu.SemaphoreType.DMA((8,)),
        ],
        compiler_params=pltpu.CompilerParams(collective_id=2, has_side_effects=True),
    )(partial_sums.reshape(SIDE, 2, OWN, norb))


def pick(index, rows, count):
    one_hot = (index[:, None] == jnp.arange(count, dtype=jnp.int32)[None, :]).astype(BF16)
    return jnp.dot(one_hot, rows, preferred_element_type=F32).astype(BF16)


def outgoing_chunks(orbitals, box_counts, owner_map, grid_rows, listed, my_box, box_total, lanes):
    per_owner = LIST // box_total
    box_ids = jnp.arange(box_total, dtype=jnp.int32)
    first_point = jnp.sum(jnp.where(box_ids < my_box, box_counts, 0))
    my_count = jnp.sum(jnp.where(box_ids == my_box, box_counts, 0))
    slot_ids = jnp.arange(SLOTS, dtype=jnp.int32)
    is_live = slot_ids < my_count
    padded = jnp.concatenate([owner_map, jnp.zeros((SLOTS,), jnp.int32)])
    position = lax.dynamic_slice(padded, (first_point,), (SLOTS,))
    owner_ids = position // OWN
    local_ids = position - owner_ids * OWN
    matches = (
        (owner_ids[:, None] == owner_ids[None, :])
        & is_live[None, :]
        & (slot_ids[None, :] < slot_ids[:, None])
    )
    pair_rank = jnp.sum(matches.astype(jnp.int32), axis=1)
    target = jnp.where(is_live, owner_ids * lanes + pair_rank, -1)
    dest = jnp.arange(box_total * lanes, dtype=jnp.int32)
    hits = target[None, :] == dest[:, None]
    coded = (grid_rows[0, :SLOTS] + 1) * OWN + local_ids
    found = jnp.sum(jnp.where(hits, coded[None, :], 0), axis=1)
    grid = found // OWN - 1
    local = jnp.where(found > 0, found - (grid + 1) * OWN, -1)
    picked = pick(grid, orbitals, orbitals.shape[0]).reshape(box_total, lanes, NORB)
    meta = jnp.stack([listed[0].reshape(box_total, per_owner), local.reshape(box_total, lanes)], axis=1)
    meta = jnp.pad(meta.astype(BF16), ((0, 0), (lanes - 2, 0), (0, NORB - per_owner)))
    row_ids = jnp.arange(lanes)[None, :, None]
    return jnp.where(row_ids < lanes - 2, picked, meta)


def shards(orbitals, coulomb, interp, box_counts, owner_map, grid_rows, listed):
    box_total = lax.axis_size("row") * lax.axis_size("col")
    lanes = LIST // box_total
    my_box = lax.axis_index("row") * lax.axis_size("col") + lax.axis_index("col")
    received = exchange(
        outgoing_chunks(orbitals, box_counts, owner_map, grid_rows, listed, my_box, box_total, lanes),
        0,
    )
    wanted = received[:, lanes - 2, :lanes].astype(jnp.int32).reshape(-1)
    local = received[:, lanes - 1, :lanes].astype(jnp.int32).reshape(-1)
    place = (local[None, :] == jnp.arange(OWN, dtype=jnp.int32)[:, None]).astype(BF16)
    owned_rows = jnp.dot(
        place, received.reshape(box_total * lanes, NORB), preferred_element_type=F32
    ).astype(BF16)
    partial_sums = project_rows(owned_rows, coulomb)
    owned_result = scatter_sums(partial_sums)
    fetched = exchange(pick(wanted, owned_result, OWN).reshape(box_total, lanes, NORB), 3)
    return -jnp.dot(interp, fetched.reshape(LIST, NORB), preferred_element_type=F32)


def solution(mesh):
    return jax.shard_map(
        shards,
        mesh=mesh,
        in_specs=(
            P(BOTH, None),
            P("row", "col"),
            P(BOTH, None),
            P(),
            P(),
            P(BOTH, None),
            P(BOTH, None),
        ),
        out_specs=P(BOTH, None),
        check_vma=False,
    )
```

```python
import jax
import jax.numpy as jnp
from jax import lax
from jax.experimental import pallas as pl
from jax.experimental.pallas import tpu as pltpu
from jax.sharding import PartitionSpec as P

NORB = 512
LIST = 1024
OWN = 256
SLOTS = 768
BOTH = ("row", "col")
F32 = jnp.float32
BF16 = jnp.bfloat16


SIDE = 4
MESH = pl.DeviceIdType.MESH


def place(me, step):
    count, cols = lax.axis_size("row") * lax.axis_size("col"), lax.axis_size("col")
    other = lax.rem(me + step, count)
    return other, (other // cols, lax.rem(other, cols))


def greet_all(me):
    count = lax.axis_size("row") * lax.axis_size("col")
    barrier = pltpu.get_barrier_semaphore()

    def signal(step, carry):
        pl.semaphore_signal(barrier, inc=1, device_id=place(me, step)[1], device_id_type=MESH)
        return carry

    lax.fori_loop(1, count, signal, 0)
    pl.semaphore_wait(barrier, count - 1)


def send_all(me, src, dst, send_sem, recv_sem, own_sem):
    count = lax.axis_size("row") * lax.axis_size("col")
    own = pltpu.make_async_copy(src.at[me], dst.at[me], own_sem)
    own.start()

    def send(step, carry):
        other, device = place(me, step)
        pltpu.make_async_remote_copy(
            src_ref=src.at[other],
            dst_ref=dst.at[me],
            send_sem=send_sem,
            recv_sem=recv_sem,
            device_id=device,
            device_id_type=MESH,
        ).start()
        return carry

    lax.fori_loop(1, count, send, 0)
    own.wait()
    many = pl.ds(0, count - 1)
    pltpu.make_async_copy(src.at[many], dst.at[many], send_sem).wait()
    pltpu.make_async_copy(src.at[many], dst.at[many], recv_sem).wait()


def exchange_kernel(src, dst, *sems):
    me = lax.axis_index("row") * lax.axis_size("col") + lax.axis_index("col")
    greet_all(me)
    send_all(me, src, dst, *sems)


def exchange(chunks, collective_id):
    return pl.pallas_call(
        exchange_kernel,
        out_shape=jax.ShapeDtypeStruct(chunks.shape, chunks.dtype),
        in_specs=[pl.BlockSpec(memory_space=pltpu.VMEM)],
        out_specs=pl.BlockSpec(memory_space=pltpu.VMEM),
        scratch_shapes=[pltpu.SemaphoreType.DMA] * 3,
        compiler_params=pltpu.CompilerParams(collective_id=collective_id, has_side_effects=True),
    )(chunks)


def around(at):
    return lax.rem(at + SIDE - 1, SIDE), lax.rem(at + 1, SIDE), lax.rem(at + 2, SIDE)


def project_kernel(
    own, coulomb, chosen, out, buf, left, tile, acc, part, inbox, stage, halves, blocks, result, outgoing,
    send_sem, recv_sem, own_sem, sum_send, sum_recv, *out_sems
):
    row, col = lax.axis_index("row"), lax.axis_index("col")
    x, y = row // SIDE, lax.rem(row, SIDE)
    z, core = col // 2, lax.rem(col, 2)
    (xm, xp, xf), (ym, yp, yf), (zm, zp, zf) = around(x), around(y), around(z)
    on_x = ((xm * SIDE + y, col), (xp * SIDE + y, col))
    on_y = ((x * SIDE + ym, col), (x * SIDE + yp, col))
    on_z = ((row, zm * 2 + core), (row, zp * 2 + core))
    mate = (row, z * 2 + 1 - core)
    used, started = [0], []
    tile_in = pltpu.make_async_copy(coulomb, tile, own_sem.at[2])
    tile_in.start()

    def push(src, dst, device, landing):
        index = used[0]
        used[0] += 1
        pair = send_sem.at[index], recv_sem.at[index]
        copy = pltpu.make_async_remote_copy(src, dst, *pair, device_id=device, device_id_type=MESH)
        copy.start()
        started.append(copy)
        return pltpu.make_async_remote_copy(landing, landing, *pair, device_id=device, device_id_type=MESH)

    def left_of(at_z, at_core):
        return left.at[at_z * 2 + at_core]

    me = row * lax.axis_size("col") + col
    greet_all(me)
    local = [pltpu.make_async_copy(own, buf.at[x, y], own_sem.at[0])]
    local += [
        pltpu.make_async_copy(own.at[:, q], left_of(z, core).at[:, pl.ds(64 * q, 64)], own_sem.at[1 + 2 * q])
        for q in range(2)
    ]
    for copy in local:
        copy.start()

    def slot(half, first, second):
        return buf.at[second, first, 0] if half == 0 else buf.at[first, second, 1]

    first_at = ((ym, y, yp, yf), (xm, x, xp, xf))
    second_at = ((xm, x, xp, xf), (ym, y, yp, yf))
    first_to, second_to = (on_y, on_x), (on_x, on_y)

    def second_send(half, first, src=None):
        minus, at, plus, _ = second_at[half]
        here = slot(half, first, at)
        src = here if src is None else src
        return (
            push(src, here, second_to[half][1], slot(half, first, minus)),
            push(src, here, second_to[half][0], slot(half, first, plus)),
        )

    def relay(ring, targets, where):
        minus, _, plus, far = ring
        one = push(where(minus).at[0], where(minus).at[0], targets[1], where(far).at[0])
        two = push(where(plus).at[1], where(plus).at[1], targets[0], where(far).at[1])
        return one, two

    first_waits = []
    for half in range(2):
        minus, at, plus, _ = first_at[half]
        here = slot(half, at, second_at[half][1])
        first_waits.append((
            push(own.at[half], here, first_to[half][1], slot(half, minus, second_at[half][1])),
            push(own.at[half], here, first_to[half][0], slot(half, plus, second_at[half][1])),
        ))
    second_waits = [[(first_at[h][1], second_send(h, first_at[h][1], own.at[h]))] for h in range(2)]
    for copy in local:
        copy.wait()
    mine = left_of(z, core)
    z_waits = (
        push(mine, mine, on_z[1], left_of(zm, core)),
        push(mine, mine, on_z[0], left_of(zp, core)),
    )
    mate_waits = [push(mine, mine, mate, left_of(z, 1 - core))]
    first_far = []
    for half in range(2):
        for wait in first_waits[half]:
            wait.wait_recv()
        at = second_at[half][1]
        first_far.append(relay(first_at[half], first_to[half], lambda f, h=half, s=at: slot(h, f, s)))
        for k in (0, 2):
            second_waits[half].append((first_at[half][k], second_send(half, first_at[half][k])))
    for wait in z_waits:
        wait.wait_recv()
    z_far = relay((zm, z, zp, zf), on_z, lambda at: left_of(at, core))
    for at in (zm, zp):
        mate_waits.append(push(left_of(at, core), left_of(at, core), mate, left_of(at, 1 - core)))
    relayed = {}

    def second_relay(half, k):
        first, waits = second_waits[half][k]
        for wait in waits:
            wait.wait_recv()
        relayed[half, k] = relay(second_at[half], second_to[half], lambda s: slot(half, first, s))

    def landed(*keys):
        for key in keys:
            for wait in relayed.pop(key):
                wait.wait_recv()

    first_step = [True]

    def project_at(at_z, one, two, start, final):
        left_rows = left[pl.ds(at_z * 2, 2)].reshape(2 * OWN, -1)
        total = None if start else acc[at_z]
        for bx, by in (one, two):
            rows = buf[bx, by].reshape(OWN, -1)
            pair = lax.dot_general(
                left_rows, rows, (((1,), (1,)), ((), ())), preferred_element_type=F32
            ).astype(BF16)
            at = pl.multiple_of((bx * SIDE + by) * OWN, OWN)
            weights = tile[pl.ds(pl.multiple_of(at_z * 2 * OWN, 2 * OWN), 2 * OWN), pl.ds(at, OWN)]
            term = jnp.dot(pair * weights, rows, preferred_element_type=F32)
            total = term if total is None else total + term
        if final:
            part[at_z] = total.astype(BF16).reshape(2, OWN, -1)
        else:
            acc[at_z] = total

    def project(one, two):
        start = first_step[0]
        first_step[0] = False

        @pl.loop(0, SIDE)
        def _(at_z):
            project_at(at_z, one, two, start, False)

    for half in range(2):
        second_relay(half, 0)
    for half in range(2):
        for wait in first_far[half]:
            wait.wait_recv()
        far = first_at[half][3]
        second_waits[half].append((far, second_send(half, far)))
    for wait in z_far:
        wait.wait_recv()
    mate_waits.append(push(left_of(zf, core), left_of(zf, core), mate, left_of(zf, 1 - core)))
    for wait in mate_waits:
        wait.wait_recv()
    tile_in.wait()
    project((x, y), (x, ym))
    second_relay(0, 1)
    second_relay(1, 1)
    project((x, yp), (xm, y))
    second_relay(0, 2)
    second_relay(1, 2)
    project((xp, y), (xm, ym))
    second_relay(0, 3)
    second_relay(1, 3)
    project((xm, yp), (xp, ym))
    landed((0, 0), (1, 0))
    project((xp, yp), (x, yf))
    landed((1, 1), (1, 2), (0, 1), (0, 2))
    project((xf, y), (xm, yf))
    project((xp, yf), (xf, ym))
    landed((0, 3), (1, 3))
    def sum_push(index, src_ref, dst_ref, device):
        copy = pltpu.make_async_remote_copy(
            src_ref, dst_ref, sum_send.at[index], sum_recv.at[index], device_id=device, device_id_type=MESH
        )
        copy.start()
        return copy

    mates = []
    for index, at in enumerate((zf, zp, zm, z)):
        project_at(at, (xf, yp), (xf, yf), False, True)
        mates.append(sum_push(index, part.at[at, 1 - core], inbox.at[at], mate))
    half = OWN // 2
    plus, minus = on_z[1], on_z[0]

    def add(at, start, size, write, *more):
        @pl.loop(0, size // STRIP)
        def _(i):
            rows = pl.ds(pl.multiple_of(start + i * STRIP, STRIP), STRIP)
            total = part[at, core, rows, :].astype(F32) + inbox[at, rows, :].astype(F32)
            for ref, shift in more:
                piece = pl.ds(pl.multiple_of(start - shift + i * STRIP, STRIP), STRIP)
                total += ref[piece, :].astype(F32)
            write[rows, :] = total.astype(BF16)

    mates[0].wait_recv()
    add(zf, 0, 2 * half, stage.at[0])
    up = sum_push(4, stage.at[0, pl.ds(0, half)], halves.at[0], plus)
    down = sum_push(5, stage.at[0, pl.ds(half, half)], halves.at[1], minus)
    mates[1].wait_recv()
    add(zp, half, half, stage.at[1])
    mates[2].wait_recv()
    add(zm, 0, half, stage.at[2])
    up.wait_recv()
    add(zp, 0, half, stage.at[1], (halves.at[0], 0))
    up_block = sum_push(6, stage.at[1], blocks.at[0], plus)
    down.wait_recv()
    add(zm, half, half, stage.at[2], (halves.at[1], half))
    down_block = sum_push(7, stage.at[2], blocks.at[1], minus)
    mates[3].wait_recv()
    up_block.wait_recv()
    down_block.wait_recv()
    add(z, 0, 2 * half, result, (blocks.at[0], 0), (blocks.at[1], 0))
    for copy in (*mates, up, down, up_block, down_block):
        copy.wait_send()
    for i in range(outgoing.shape[0] * outgoing.shape[1] // OWN):
        boxes = OWN // outgoing.shape[1]
        picked = jnp.dot(chosen[pl.ds(i * OWN, OWN), :], result[...], preferred_element_type=F32)
        outgoing[pl.ds(i * boxes, boxes)] = picked.reshape(boxes, outgoing.shape[1], -1).astype(BF16)
    send_all(me, outgoing, out, *out_sems)
    for copy in started:
        copy.wait_send()


STRIP = 32
COPIES = 2 * (4 + 4 * 4) + 4 + 4


def project_rows(owned_rows, coulomb, chosen, boxes):
    rows, norb = owned_rows.shape
    own = owned_rows.reshape(2, 2, rows // 4, norb)
    out = (boxes, chosen.shape[0] // boxes, norb)
    vmem = pl.BlockSpec(memory_space=pltpu.VMEM)
    return pl.pallas_call(
        project_kernel,
        out_shape=jax.ShapeDtypeStruct(out, BF16),
        in_specs=[vmem, pl.BlockSpec(memory_space=pl.ANY), vmem],
        out_specs=vmem,
        scratch_shapes=[
            pltpu.VMEM((SIDE, SIDE, *own.shape), BF16),
            pltpu.VMEM((SIDE * 2, 2, rows // 2, norb), BF16),
            pltpu.VMEM(coulomb.shape, BF16),
            pltpu.VMEM((SIDE, 2 * rows, norb), F32),
            pltpu.VMEM((SIDE, 2, rows, norb), BF16),
            pltpu.VMEM((SIDE, rows, norb), BF16),
            pltpu.VMEM((3, rows, norb), BF16),
            pltpu.VMEM((2, rows // 2, norb), BF16),
            pltpu.VMEM((2, rows, norb), BF16),
            pltpu.VMEM((rows, norb), BF16),
            pltpu.VMEM(out, BF16),
            pltpu.SemaphoreType.DMA((COPIES,)),
            pltpu.SemaphoreType.DMA((COPIES,)),
            pltpu.SemaphoreType.DMA((4,)),
            pltpu.SemaphoreType.DMA((8,)),
            pltpu.SemaphoreType.DMA((8,)),
            *[pltpu.SemaphoreType.DMA] * 3,
        ],
        compiler_params=pltpu.CompilerParams(
            collective_id=1, has_side_effects=True, vmem_limit_bytes=56 * 1024 * 1024
        ),
    )(own, coulomb, chosen)


def pick(index, rows, count):
    one_hot = (index[:, None] == jnp.arange(count, dtype=jnp.int32)[None, :]).astype(BF16)
    return jnp.dot(one_hot, rows, preferred_element_type=F32).astype(BF16)


def outgoing_chunks(orbitals, box_counts, owner_map, grid_rows, listed, my_box, box_total, lanes):
    per_owner = LIST // box_total
    box_ids = jnp.arange(box_total, dtype=jnp.int32)
    first_point = jnp.sum(jnp.where(box_ids < my_box, box_counts, 0))
    my_count = jnp.sum(jnp.where(box_ids == my_box, box_counts, 0))
    slot_ids = jnp.arange(SLOTS, dtype=jnp.int32)
    is_live = slot_ids < my_count
    padded = jnp.concatenate([owner_map, jnp.zeros((SLOTS,), jnp.int32)])
    position = lax.dynamic_slice(padded, (first_point,), (SLOTS,))
    owner_ids = position // OWN
    local_ids = position - owner_ids * OWN
    matches = (
        (owner_ids[:, None] == owner_ids[None, :])
        & is_live[None, :]
        & (slot_ids[None, :] < slot_ids[:, None])
    )
    pair_rank = jnp.sum(matches.astype(jnp.int32), axis=1)
    target = jnp.where(is_live, owner_ids * lanes + pair_rank, -1)
    dest = jnp.arange(box_total * lanes, dtype=jnp.int32)
    hits = target[None, :] == dest[:, None]
    coded = (grid_rows[0, :SLOTS] + 1) * OWN + local_ids
    found = jnp.sum(jnp.where(hits, coded[None, :], 0), axis=1)
    grid = found // OWN - 1
    local = jnp.where(found > 0, found - (grid + 1) * OWN, -1)
    picked = pick(grid, orbitals, orbitals.shape[0]).reshape(box_total, lanes, NORB)
    meta = jnp.stack([listed[0].reshape(box_total, per_owner), local.reshape(box_total, lanes)], axis=1)
    meta = jnp.pad(meta.astype(BF16), ((0, 0), (lanes - 2, 0), (0, NORB - per_owner)))
    row_ids = jnp.arange(lanes)[None, :, None]
    return jnp.where(row_ids < lanes - 2, picked, meta)


def shards(orbitals, coulomb, interp, box_counts, owner_map, grid_rows, listed):
    box_total = lax.axis_size("row") * lax.axis_size("col")
    lanes = LIST // box_total
    my_box = lax.axis_index("row") * lax.axis_size("col") + lax.axis_index("col")
    received = exchange(
        outgoing_chunks(orbitals, box_counts, owner_map, grid_rows, listed, my_box, box_total, lanes),
        0,
    )
    wanted = received[:, lanes - 2, :lanes].astype(jnp.int32).reshape(-1)
    local = received[:, lanes - 1, :lanes].astype(jnp.int32).reshape(-1)
    place = (local[None, :] == jnp.arange(OWN, dtype=jnp.int32)[:, None]).astype(BF16)
    owned_rows = jnp.dot(
        place, received.reshape(box_total * lanes, NORB), preferred_element_type=F32
    ).astype(BF16)
    chosen = (wanted[:, None] == jnp.arange(OWN, dtype=jnp.int32)[None, :]).astype(BF16)
    fetched = project_rows(owned_rows, coulomb, chosen, box_total)
    return -jnp.dot(interp, fetched.reshape(LIST, NORB), preferred_element_type=F32)


def solution(mesh):
    return jax.shard_map(
        shards,
        mesh=mesh,
        in_specs=(
            P(BOTH, None),
            P("row", "col"),
            P(BOTH, None),
            P(),
            P(),
            P(BOTH, None),
            P(BOTH, None),
        ),
        out_specs=P(BOTH, None),
        check_vma=False,
    )
```

```python
import jax
import jax.numpy as jnp
from jax import lax
from jax.experimental import pallas as pl
from jax.experimental.pallas import tpu as pltpu
from jax.sharding import PartitionSpec as P

NORB = 512
LIST = 1024
OWN = 256
SLOTS = 768
BOTH = ("row", "col")
F32 = jnp.float32
BF16 = jnp.bfloat16


SIDE = 4
STRIDE = 37
MESH = pl.DeviceIdType.MESH


def place(me, step):
    count, cols = lax.axis_size("row") * lax.axis_size("col"), lax.axis_size("col")
    other = lax.rem(me + STRIDE * step, count)
    return other, (other // cols, lax.rem(other, cols))


def greet_all(me):
    count = lax.axis_size("row") * lax.axis_size("col")
    barrier = pltpu.get_barrier_semaphore()

    def signal(step, carry):
        pl.semaphore_signal(barrier, inc=1, device_id=place(me, step)[1], device_id_type=MESH)
        return carry

    lax.fori_loop(1, count, signal, 0)
    pl.semaphore_wait(barrier, count - 1)


def send_all(me, src, dst, send_sem, recv_sem, own_sem):
    count = lax.axis_size("row") * lax.axis_size("col")
    own = pltpu.make_async_copy(src.at[me], dst.at[me], own_sem)
    own.start()

    def send(step, carry):
        other, device = place(me, step)
        pltpu.make_async_remote_copy(
            src_ref=src.at[other],
            dst_ref=dst.at[me],
            send_sem=send_sem,
            recv_sem=recv_sem,
            device_id=device,
            device_id_type=MESH,
        ).start()
        return carry

    lax.fori_loop(1, count, send, 0)
    own.wait()
    many = pl.ds(0, count - 1)
    pltpu.make_async_copy(src.at[many], dst.at[many], send_sem).wait()
    pltpu.make_async_copy(src.at[many], dst.at[many], recv_sem).wait()


def exchange_kernel(src, dst, *sems):
    me = lax.axis_index("row") * lax.axis_size("col") + lax.axis_index("col")
    greet_all(me)
    send_all(me, src, dst, *sems)


def exchange(chunks, collective_id):
    return pl.pallas_call(
        exchange_kernel,
        out_shape=jax.ShapeDtypeStruct(chunks.shape, chunks.dtype),
        in_specs=[pl.BlockSpec(memory_space=pltpu.VMEM)],
        out_specs=pl.BlockSpec(memory_space=pltpu.VMEM),
        scratch_shapes=[pltpu.SemaphoreType.DMA] * 3,
        compiler_params=pltpu.CompilerParams(collective_id=collective_id, has_side_effects=True),
    )(chunks)


def around(at):
    return lax.rem(at + SIDE - 1, SIDE), lax.rem(at + 1, SIDE), lax.rem(at + 2, SIDE)


def project_kernel(
    own, coulomb, chosen, out, buf, left, tile, acc, part, inbox, stage, halves, blocks, result, outgoing,
    send_sem, recv_sem, own_sem, sum_send, sum_recv, *out_sems
):
    row, col = lax.axis_index("row"), lax.axis_index("col")
    x, y = row // SIDE, lax.rem(row, SIDE)
    z, core = col // 2, lax.rem(col, 2)
    (xm, xp, xf), (ym, yp, yf), (zm, zp, zf) = around(x), around(y), around(z)
    on_x = ((xm * SIDE + y, col), (xp * SIDE + y, col))
    on_y = ((x * SIDE + ym, col), (x * SIDE + yp, col))
    on_z = ((row, zm * 2 + core), (row, zp * 2 + core))
    mate = (row, z * 2 + 1 - core)
    used, started = [0], []
    tile_in = pltpu.make_async_copy(coulomb, tile, own_sem.at[2])
    tile_in.start()

    def push(src, dst, device, landing):
        index = used[0]
        used[0] += 1
        pair = send_sem.at[index], recv_sem.at[index]
        copy = pltpu.make_async_remote_copy(src, dst, *pair, device_id=device, device_id_type=MESH)
        copy.start()
        started.append(copy)
        return pltpu.make_async_remote_copy(landing, landing, *pair, device_id=device, device_id_type=MESH)

    def left_of(at_z, at_core):
        return left.at[at_z * 2 + at_core]

    me = row * lax.axis_size("col") + col
    greet_all(me)
    local = [pltpu.make_async_copy(own, buf.at[x, y], own_sem.at[0])]
    local += [
        pltpu.make_async_copy(own.at[:, q], left_of(z, core).at[:, pl.ds(64 * q, 64)], own_sem.at[1 + 2 * q])
        for q in range(2)
    ]
    for copy in local:
        copy.start()

    def slot(half, first, second):
        return buf.at[second, first, 0] if half == 0 else buf.at[first, second, 1]

    first_at = ((ym, y, yp, yf), (xm, x, xp, xf))
    second_at = ((xm, x, xp, xf), (ym, y, yp, yf))
    first_to, second_to = (on_y, on_x), (on_x, on_y)

    def second_send(half, first, src=None):
        minus, at, plus, _ = second_at[half]
        here = slot(half, first, at)
        src = here if src is None else src
        return (
            push(src, here, second_to[half][1], slot(half, first, minus)),
            push(src, here, second_to[half][0], slot(half, first, plus)),
        )

    def relay(ring, targets, where):
        minus, _, plus, far = ring
        one = push(where(minus).at[0], where(minus).at[0], targets[1], where(far).at[0])
        two = push(where(plus).at[1], where(plus).at[1], targets[0], where(far).at[1])
        return one, two

    first_waits = []
    for half in range(2):
        minus, at, plus, _ = first_at[half]
        here = slot(half, at, second_at[half][1])
        first_waits.append((
            push(own.at[half], here, first_to[half][1], slot(half, minus, second_at[half][1])),
            push(own.at[half], here, first_to[half][0], slot(half, plus, second_at[half][1])),
        ))
    second_waits = [[(first_at[h][1], second_send(h, first_at[h][1], own.at[h]))] for h in range(2)]
    for copy in local:
        copy.wait()
    mine = left_of(z, core)
    z_waits = (
        push(mine, mine, on_z[1], left_of(zm, core)),
        push(mine, mine, on_z[0], left_of(zp, core)),
    )
    mate_waits = [push(mine, mine, mate, left_of(z, 1 - core))]
    first_far = []
    for half in range(2):
        for wait in first_waits[half]:
            wait.wait_recv()
        at = second_at[half][1]
        first_far.append(relay(first_at[half], first_to[half], lambda f, h=half, s=at: slot(h, f, s)))
        for k in (0, 2):
            second_waits[half].append((first_at[half][k], second_send(half, first_at[half][k])))
    for wait in z_waits:
        wait.wait_recv()
    z_far = relay((zm, z, zp, zf), on_z, lambda at: left_of(at, core))
    for at in (zm, zp):
        mate_waits.append(push(left_of(at, core), left_of(at, core), mate, left_of(at, 1 - core)))
    relayed = {}

    def second_relay(half, k):
        first, waits = second_waits[half][k]
        for wait in waits:
            wait.wait_recv()
        relayed[half, k] = relay(second_at[half], second_to[half], lambda s: slot(half, first, s))

    def landed(*keys):
        for key in keys:
            for wait in relayed.pop(key):
                wait.wait_recv()

    first_step = [True]

    def project_at(at_z, one, two, start, final):
        left_rows = left[pl.ds(at_z * 2, 2)].reshape(2 * OWN, -1)
        total = None if start else acc[at_z]
        for bx, by in (one, two):
            rows = buf[bx, by].reshape(OWN, -1)
            pair = lax.dot_general(
                left_rows, rows, (((1,), (1,)), ((), ())), preferred_element_type=F32
            ).astype(BF16)
            at = pl.multiple_of((bx * SIDE + by) * OWN, OWN)
            weights = tile[pl.ds(pl.multiple_of(at_z * 2 * OWN, 2 * OWN), 2 * OWN), pl.ds(at, OWN)]
            term = jnp.dot(pair * weights, rows, preferred_element_type=F32)
            total = term if total is None else total + term
        if final:
            part[at_z] = total.astype(BF16).reshape(2, OWN, -1)
        else:
            acc[at_z] = total

    def project(one, two):
        start = first_step[0]
        first_step[0] = False

        @pl.loop(0, SIDE)
        def _(at_z):
            project_at(at_z, one, two, start, False)

    for half in range(2):
        second_relay(half, 0)
    for half in range(2):
        for wait in first_far[half]:
            wait.wait_recv()
        far = first_at[half][3]
        second_waits[half].append((far, second_send(half, far)))
    for wait in z_far:
        wait.wait_recv()
    mate_waits.append(push(left_of(zf, core), left_of(zf, core), mate, left_of(zf, 1 - core)))
    for wait in mate_waits:
        wait.wait_recv()
    tile_in.wait()
    project((x, y), (x, ym))
    for k in (1, 2):
        second_relay(0, k)
        second_relay(1, k)
    project((x, yp), (xm, y))
    second_relay(0, 3)
    second_relay(1, 3)
    project((xp, y), (xm, ym))
    project((xm, yp), (xp, ym))
    landed((0, 0), (1, 0))
    project((xp, yp), (x, yf))
    landed((1, 1), (1, 2), (0, 1), (0, 2))
    project((xf, y), (xm, yf))
    project((xp, yf), (xf, ym))
    landed((0, 3), (1, 3))
    def sum_push(index, src_ref, dst_ref, device):
        copy = pltpu.make_async_remote_copy(
            src_ref, dst_ref, sum_send.at[index], sum_recv.at[index], device_id=device, device_id_type=MESH
        )
        copy.start()
        return copy

    mates = []
    for index, at in enumerate((zf, zp, zm, z)):
        project_at(at, (xf, yp), (xf, yf), False, True)
        mates.append(sum_push(index, part.at[at, 1 - core], inbox.at[at], mate))
    half = OWN // 2
    plus, minus = on_z[1], on_z[0]

    def add(at, start, size, write, *more):
        @pl.loop(0, size // STRIP)
        def _(i):
            rows = pl.ds(pl.multiple_of(start + i * STRIP, STRIP), STRIP)
            total = part[at, core, rows, :].astype(F32) + inbox[at, rows, :].astype(F32)
            for ref, shift in more:
                piece = pl.ds(pl.multiple_of(start - shift + i * STRIP, STRIP), STRIP)
                total += ref[piece, :].astype(F32)
            write[rows, :] = total.astype(BF16)

    mates[0].wait_recv()
    add(zf, 0, 2 * half, stage.at[0])
    up = sum_push(4, stage.at[0, pl.ds(0, half)], halves.at[0], plus)
    down = sum_push(5, stage.at[0, pl.ds(half, half)], halves.at[1], minus)
    mates[1].wait_recv()
    add(zp, half, half, stage.at[1])
    mates[2].wait_recv()
    add(zm, 0, half, stage.at[2])
    up.wait_recv()
    add(zp, 0, half, stage.at[1], (halves.at[0], 0))
    up_block = sum_push(6, stage.at[1], blocks.at[0], plus)
    down.wait_recv()
    add(zm, half, half, stage.at[2], (halves.at[1], half))
    down_block = sum_push(7, stage.at[2], blocks.at[1], minus)
    mates[3].wait_recv()
    up_block.wait_recv()
    down_block.wait_recv()
    add(z, 0, 2 * half, result, (blocks.at[0], 0), (blocks.at[1], 0))
    for copy in (*mates, up, down, up_block, down_block):
        copy.wait_send()
    for i in range(outgoing.shape[0] * outgoing.shape[1] // OWN):
        boxes = OWN // outgoing.shape[1]
        picked = jnp.dot(chosen[pl.ds(i * OWN, OWN), :], result[...], preferred_element_type=F32)
        outgoing[pl.ds(i * boxes, boxes)] = picked.reshape(boxes, outgoing.shape[1], -1).astype(BF16)
    send_all(me, outgoing, out, *out_sems)
    for copy in started:
        copy.wait_send()


STRIP = 32
COPIES = 2 * (4 + 4 * 4) + 4 + 4


def project_rows(owned_rows, coulomb, chosen, boxes):
    rows, norb = owned_rows.shape
    own = owned_rows.reshape(2, 2, rows // 4, norb)
    out = (boxes, chosen.shape[0] // boxes, norb)
    vmem = pl.BlockSpec(memory_space=pltpu.VMEM)
    return pl.pallas_call(
        project_kernel,
        out_shape=jax.ShapeDtypeStruct(out, BF16),
        in_specs=[vmem, pl.BlockSpec(memory_space=pl.ANY), vmem],
        out_specs=vmem,
        scratch_shapes=[
            pltpu.VMEM((SIDE, SIDE, *own.shape), BF16),
            pltpu.VMEM((SIDE * 2, 2, rows // 2, norb), BF16),
            pltpu.VMEM(coulomb.shape, BF16),
            pltpu.VMEM((SIDE, 2 * rows, norb), F32),
            pltpu.VMEM((SIDE, 2, rows, norb), BF16),
            pltpu.VMEM((SIDE, rows, norb), BF16),
            pltpu.VMEM((3, rows, norb), BF16),
            pltpu.VMEM((2, rows // 2, norb), BF16),
            pltpu.VMEM((2, rows, norb), BF16),
            pltpu.VMEM((rows, norb), BF16),
            pltpu.VMEM(out, BF16),
            pltpu.SemaphoreType.DMA((COPIES,)),
            pltpu.SemaphoreType.DMA((COPIES,)),
            pltpu.SemaphoreType.DMA((4,)),
            pltpu.SemaphoreType.DMA((8,)),
            pltpu.SemaphoreType.DMA((8,)),
            *[pltpu.SemaphoreType.DMA] * 3,
        ],
        compiler_params=pltpu.CompilerParams(
            collective_id=1, has_side_effects=True, vmem_limit_bytes=56 * 1024 * 1024
        ),
    )(own, coulomb, chosen)


def action_kernel(interp, rows, out):
    out[...] = -jnp.dot(interp[...], rows[...], preferred_element_type=F32)


def action(interp, rows):
    count, listed = interp.shape
    norb = rows.shape[1]
    block = count // 4
    return pl.pallas_call(
        action_kernel,
        grid=(4,),
        out_shape=jax.ShapeDtypeStruct((count, norb), F32),
        in_specs=[pl.BlockSpec((block, listed), lambda i: (i, 0)), pl.BlockSpec((listed, norb), lambda i: (0, 0))],
        out_specs=pl.BlockSpec((block, norb), lambda i: (i, 0)),
    )(interp, rows)


def pick(index, rows, count):
    one_hot = (index[:, None] == jnp.arange(count, dtype=jnp.int32)[None, :]).astype(BF16)
    return jnp.dot(one_hot, rows, preferred_element_type=F32).astype(BF16)


def outgoing_chunks(orbitals, box_counts, owner_map, grid_rows, listed, my_box, box_total, lanes):
    per_owner = LIST // box_total
    box_ids = jnp.arange(box_total, dtype=jnp.int32)
    first_point = jnp.sum(jnp.where(box_ids < my_box, box_counts, 0))
    my_count = jnp.sum(jnp.where(box_ids == my_box, box_counts, 0))
    slot_ids = jnp.arange(SLOTS, dtype=jnp.int32)
    is_live = slot_ids < my_count
    padded = jnp.concatenate([owner_map, jnp.zeros((SLOTS,), jnp.int32)])
    position = lax.dynamic_slice(padded, (first_point,), (SLOTS,))
    owner_ids = position // OWN
    local_ids = position - owner_ids * OWN
    matches = (
        (owner_ids[:, None] == owner_ids[None, :])
        & is_live[None, :]
        & (slot_ids[None, :] < slot_ids[:, None])
    )
    pair_rank = jnp.sum(matches.astype(jnp.int32), axis=1)
    target = jnp.where(is_live, owner_ids * lanes + pair_rank, -1)
    dest = jnp.arange(box_total * lanes, dtype=jnp.int32)
    hits = target[None, :] == dest[:, None]
    coded = (grid_rows[0, :SLOTS] + 1) * OWN + local_ids
    found = jnp.sum(jnp.where(hits, coded[None, :], 0), axis=1)
    grid = found // OWN - 1
    local = jnp.where(found > 0, found - (grid + 1) * OWN, -1)
    picked = pick(grid, orbitals, orbitals.shape[0]).reshape(box_total, lanes, NORB)
    meta = jnp.stack([listed[0].reshape(box_total, per_owner), local.reshape(box_total, lanes)], axis=1)
    meta = jnp.pad(meta.astype(BF16), ((0, 0), (lanes - 2, 0), (0, NORB - per_owner)))
    row_ids = jnp.arange(lanes)[None, :, None]
    return jnp.where(row_ids < lanes - 2, picked, meta)


def shards(orbitals, coulomb, interp, box_counts, owner_map, grid_rows, listed):
    box_total = lax.axis_size("row") * lax.axis_size("col")
    lanes = LIST // box_total
    my_box = lax.axis_index("row") * lax.axis_size("col") + lax.axis_index("col")
    received = exchange(
        outgoing_chunks(orbitals, box_counts, owner_map, grid_rows, listed, my_box, box_total, lanes),
        0,
    )
    wanted = received[:, lanes - 2, :lanes].astype(jnp.int32).reshape(-1)
    local = received[:, lanes - 1, :lanes].astype(jnp.int32).reshape(-1)
    place = (local[None, :] == jnp.arange(OWN, dtype=jnp.int32)[:, None]).astype(BF16)
    owned_rows = jnp.dot(
        place, received.reshape(box_total * lanes, NORB), preferred_element_type=F32
    ).astype(BF16)
    chosen = (wanted[:, None] == jnp.arange(OWN, dtype=jnp.int32)[None, :]).astype(BF16)
    fetched = project_rows(owned_rows, coulomb, chosen, box_total)
    return action(interp, fetched.reshape(LIST, NORB))


def solution(mesh):
    return jax.shard_map(
        shards,
        mesh=mesh,
        in_specs=(
            P(BOTH, None),
            P("row", "col"),
            P(BOTH, None),
            P(),
            P(),
            P(BOTH, None),
            P(BOTH, None),
        ),
        out_specs=P(BOTH, None),
        check_vma=False,
    )
```

```python
import jax
import jax.numpy as jnp
from jax import lax
from jax.experimental import pallas as pl
from jax.experimental.pallas import tpu as pltpu
from jax.sharding import PartitionSpec as P

NORB = 512
LIST = 1024
OWN = 256
SLOTS = 768
BOTH = ("row", "col")
F32 = jnp.float32
BF16 = jnp.bfloat16


SIDE = 4
STRIDE = 37
MESH = pl.DeviceIdType.MESH


def place(me, step):
    count, cols = lax.axis_size("row") * lax.axis_size("col"), lax.axis_size("col")
    other = lax.rem(me + STRIDE * step, count)
    return other, (other // cols, lax.rem(other, cols))


def greet_all(me, meanwhile=None):
    count = lax.axis_size("row") * lax.axis_size("col")
    barrier = pltpu.get_barrier_semaphore()

    def signal(step, carry):
        pl.semaphore_signal(barrier, inc=1, device_id=place(me, step)[1], device_id_type=MESH)
        return carry

    lax.fori_loop(1, count, signal, 0)
    if meanwhile is not None:
        meanwhile()
    pl.semaphore_wait(barrier, count - 1)


def send_all(me, src, dst, send_sem, recv_sem, own_sem):
    count = lax.axis_size("row") * lax.axis_size("col")
    own = pltpu.make_async_copy(src.at[me], dst.at[me], own_sem)
    own.start()

    def send(step, carry):
        other, device = place(me, step)
        pltpu.make_async_remote_copy(
            src_ref=src.at[other],
            dst_ref=dst.at[me],
            send_sem=send_sem,
            recv_sem=recv_sem,
            device_id=device,
            device_id_type=MESH,
        ).start()
        return carry

    lax.fori_loop(1, count, send, 0)
    own.wait()
    many = pl.ds(0, count - 1)
    pltpu.make_async_copy(src.at[many], dst.at[many], send_sem).wait()
    pltpu.make_async_copy(src.at[many], dst.at[many], recv_sem).wait()


def exchange_kernel(index, rows, meta, dst, src, *sems):
    me = lax.axis_index("row") * lax.axis_size("col") + lax.axis_index("col")
    boxes = OWN // src.shape[1]

    def fill():
        for i in range(index.shape[0] // OWN):
            places = lax.broadcasted_iota(jnp.int32, (OWN, rows.shape[0]), 1)
            one_hot = (index[pl.ds(i * OWN, OWN), :] == places).astype(F32).astype(BF16)
            picked = jnp.dot(one_hot, rows[...], preferred_element_type=F32)
            at = pl.ds(i * boxes, boxes)
            src[at] = (picked.reshape(boxes, src.shape[1], -1) + meta[at].astype(F32)).astype(BF16)

    greet_all(me, fill)
    send_all(me, src, dst, *sems)


def exchange(index, rows, meta):
    return pl.pallas_call(
        exchange_kernel,
        out_shape=jax.ShapeDtypeStruct(meta.shape, meta.dtype),
        in_specs=[pl.BlockSpec(memory_space=pltpu.VMEM)] * 3,
        out_specs=pl.BlockSpec(memory_space=pltpu.VMEM),
        scratch_shapes=[pltpu.VMEM(meta.shape, meta.dtype)] + [pltpu.SemaphoreType.DMA] * 3,
        compiler_params=pltpu.CompilerParams(collective_id=0, has_side_effects=True),
    )(index[:, None], rows, meta)


def around(at):
    return lax.rem(at + SIDE - 1, SIDE), lax.rem(at + 1, SIDE), lax.rem(at + 2, SIDE)


def project_kernel(
    own, coulomb, chosen, out, buf, left, tile, acc, part, inbox, stage, halves, blocks, result, outgoing,
    send_sem, recv_sem, own_sem, sum_send, sum_recv, *out_sems
):
    row, col = lax.axis_index("row"), lax.axis_index("col")
    x, y = row // SIDE, lax.rem(row, SIDE)
    z, core = col // 2, lax.rem(col, 2)
    (xm, xp, xf), (ym, yp, yf), (zm, zp, zf) = around(x), around(y), around(z)
    on_x = ((xm * SIDE + y, col), (xp * SIDE + y, col))
    on_y = ((x * SIDE + ym, col), (x * SIDE + yp, col))
    on_z = ((row, zm * 2 + core), (row, zp * 2 + core))
    mate = (row, z * 2 + 1 - core)
    used, started = [0], []
    tile_in = pltpu.make_async_copy(coulomb, tile, own_sem.at[2])
    tile_in.start()

    def push(src, dst, device, landing):
        index = used[0]
        used[0] += 1
        pair = send_sem.at[index], recv_sem.at[index]
        copy = pltpu.make_async_remote_copy(src, dst, *pair, device_id=device, device_id_type=MESH)
        copy.start()
        started.append(copy)
        return pltpu.make_async_remote_copy(landing, landing, *pair, device_id=device, device_id_type=MESH)

    def left_of(at_z, at_core):
        return left.at[at_z * 2 + at_core]

    me = row * lax.axis_size("col") + col
    greet_all(me)
    local = [pltpu.make_async_copy(own, buf.at[x, y], own_sem.at[0])]
    local += [
        pltpu.make_async_copy(own.at[:, q], left_of(z, core).at[:, pl.ds(64 * q, 64)], own_sem.at[1 + 2 * q])
        for q in range(2)
    ]
    for copy in local:
        copy.start()

    def slot(half, first, second):
        return buf.at[second, first, 0] if half == 0 else buf.at[first, second, 1]

    first_at = ((ym, y, yp, yf), (xm, x, xp, xf))
    second_at = ((xm, x, xp, xf), (ym, y, yp, yf))
    first_to, second_to = (on_y, on_x), (on_x, on_y)

    def second_send(half, first, src=None):
        minus, at, plus, _ = second_at[half]
        here = slot(half, first, at)
        src = here if src is None else src
        return (
            push(src, here, second_to[half][1], slot(half, first, minus)),
            push(src, here, second_to[half][0], slot(half, first, plus)),
        )

    def relay(ring, targets, where):
        minus, _, plus, far = ring
        one = push(where(minus).at[0], where(minus).at[0], targets[1], where(far).at[0])
        two = push(where(plus).at[1], where(plus).at[1], targets[0], where(far).at[1])
        return one, two

    first_waits = []
    for half in range(2):
        minus, at, plus, _ = first_at[half]
        here = slot(half, at, second_at[half][1])
        first_waits.append((
            push(own.at[half], here, first_to[half][1], slot(half, minus, second_at[half][1])),
            push(own.at[half], here, first_to[half][0], slot(half, plus, second_at[half][1])),
        ))
    second_waits = [[(first_at[h][1], second_send(h, first_at[h][1], own.at[h]))] for h in range(2)]
    for copy in local:
        copy.wait()
    mine = left_of(z, core)
    z_waits = (
        push(mine, mine, on_z[1], left_of(zm, core)),
        push(mine, mine, on_z[0], left_of(zp, core)),
    )
    mate_waits = [push(mine, mine, mate, left_of(z, 1 - core))]
    first_far = []
    for half in range(2):
        for wait in first_waits[half]:
            wait.wait_recv()
        at = second_at[half][1]
        first_far.append(relay(first_at[half], first_to[half], lambda f, h=half, s=at: slot(h, f, s)))
        for k in (0, 2):
            second_waits[half].append((first_at[half][k], second_send(half, first_at[half][k])))
    for wait in z_waits:
        wait.wait_recv()
    z_far = relay((zm, z, zp, zf), on_z, lambda at: left_of(at, core))
    for at in (zm, zp):
        mate_waits.append(push(left_of(at, core), left_of(at, core), mate, left_of(at, 1 - core)))
    relayed = {}

    def second_relay(half, k):
        first, waits = second_waits[half][k]
        for wait in waits:
            wait.wait_recv()
        relayed[half, k] = relay(second_at[half], second_to[half], lambda s: slot(half, first, s))

    def landed(*keys):
        for key in keys:
            for wait in relayed.pop(key):
                wait.wait_recv()

    first_step = [True]

    def project_at(at_z, one, two, start, final):
        left_rows = left[pl.ds(at_z * 2, 2)].reshape(2 * OWN, -1)
        total = None if start else acc[at_z]
        for bx, by in (one, two):
            rows = buf[bx, by].reshape(OWN, -1)
            pair = lax.dot_general(
                left_rows, rows, (((1,), (1,)), ((), ())), preferred_element_type=F32
            ).astype(BF16)
            at = pl.multiple_of((bx * SIDE + by) * OWN, OWN)
            weights = tile[pl.ds(pl.multiple_of(at_z * 2 * OWN, 2 * OWN), 2 * OWN), pl.ds(at, OWN)]
            term = jnp.dot(pair * weights, rows, preferred_element_type=F32)
            total = term if total is None else total + term
        if final:
            part[at_z] = total.astype(BF16).reshape(2, OWN, -1)
        else:
            acc[at_z] = total

    def project(one, two):
        start = first_step[0]
        first_step[0] = False

        @pl.loop(0, SIDE)
        def _(at_z):
            project_at(at_z, one, two, start, False)

    for half in range(2):
        second_relay(half, 0)
    for half in range(2):
        for wait in first_far[half]:
            wait.wait_recv()
        far = first_at[half][3]
        second_waits[half].append((far, second_send(half, far)))
    for wait in z_far:
        wait.wait_recv()
    mate_waits.append(push(left_of(zf, core), left_of(zf, core), mate, left_of(zf, 1 - core)))
    for wait in mate_waits:
        wait.wait_recv()
    tile_in.wait()
    project((x, y), (x, ym))
    for k in (1, 2):
        second_relay(0, k)
        second_relay(1, k)
    project((x, yp), (xm, y))
    second_relay(0, 3)
    second_relay(1, 3)
    project((xp, y), (xm, ym))
    project((xm, yp), (xp, ym))
    landed((0, 0), (1, 0))
    project((xp, yp), (x, yf))
    landed((1, 1), (1, 2), (0, 1), (0, 2))
    project((xf, y), (xm, yf))
    project((xp, yf), (xf, ym))
    landed((0, 3), (1, 3))
    def sum_push(index, src_ref, dst_ref, device):
        copy = pltpu.make_async_remote_copy(
            src_ref, dst_ref, sum_send.at[index], sum_recv.at[index], device_id=device, device_id_type=MESH
        )
        copy.start()
        return copy

    mates = []
    for index, at in enumerate((zf, zp, zm, z)):
        project_at(at, (xf, yp), (xf, yf), False, True)
        mates.append(sum_push(index, part.at[at, 1 - core], inbox.at[at], mate))
    half = OWN // 2
    plus, minus = on_z[1], on_z[0]

    def add(at, start, size, write, *more):
        @pl.loop(0, size // STRIP)
        def _(i):
            rows = pl.ds(pl.multiple_of(start + i * STRIP, STRIP), STRIP)
            total = part[at, core, rows, :].astype(F32) + inbox[at, rows, :].astype(F32)
            for ref, shift in more:
                piece = pl.ds(pl.multiple_of(start - shift + i * STRIP, STRIP), STRIP)
                total += ref[piece, :].astype(F32)
            write[rows, :] = total.astype(BF16)

    mates[0].wait_recv()
    add(zf, 0, 2 * half, stage.at[0])
    up = sum_push(4, stage.at[0, pl.ds(0, half)], halves.at[0], plus)
    down = sum_push(5, stage.at[0, pl.ds(half, half)], halves.at[1], minus)
    mates[1].wait_recv()
    add(zp, half, half, stage.at[1])
    mates[2].wait_recv()
    add(zm, 0, half, stage.at[2])
    up.wait_recv()
    add(zp, 0, half, stage.at[1], (halves.at[0], 0))
    up_block = sum_push(6, stage.at[1], blocks.at[0], plus)
    down.wait_recv()
    add(zm, half, half, stage.at[2], (halves.at[1], half))
    down_block = sum_push(7, stage.at[2], blocks.at[1], minus)
    mates[3].wait_recv()
    up_block.wait_recv()
    down_block.wait_recv()
    add(z, 0, 2 * half, result, (blocks.at[0], 0), (blocks.at[1], 0))
    for copy in (*mates, up, down, up_block, down_block):
        copy.wait_send()
    for i in range(outgoing.shape[0] * outgoing.shape[1] // OWN):
        boxes = OWN // outgoing.shape[1]
        picked = jnp.dot(chosen[pl.ds(i * OWN, OWN), :], result[...], preferred_element_type=F32)
        outgoing[pl.ds(i * boxes, boxes)] = picked.reshape(boxes, outgoing.shape[1], -1).astype(BF16)
    send_all(me, outgoing, out, *out_sems)
    for copy in started:
        copy.wait_send()


STRIP = 32
COPIES = 2 * (4 + 4 * 4) + 4 + 4


def project_rows(owned_rows, coulomb, chosen, boxes):
    rows, norb = owned_rows.shape
    own = owned_rows.reshape(2, 2, rows // 4, norb)
    out = (boxes, chosen.shape[0] // boxes, norb)
    vmem = pl.BlockSpec(memory_space=pltpu.VMEM)
    return pl.pallas_call(
        project_kernel,
        out_shape=jax.ShapeDtypeStruct(out, BF16),
        in_specs=[vmem, pl.BlockSpec(memory_space=pl.ANY), vmem],
        out_specs=vmem,
        scratch_shapes=[
            pltpu.VMEM((SIDE, SIDE, *own.shape), BF16),
            pltpu.VMEM((SIDE * 2, 2, rows // 2, norb), BF16),
            pltpu.VMEM(coulomb.shape, BF16),
            pltpu.VMEM((SIDE, 2 * rows, norb), F32),
            pltpu.VMEM((SIDE, 2, rows, norb), BF16),
            pltpu.VMEM((SIDE, rows, norb), BF16),
            pltpu.VMEM((3, rows, norb), BF16),
            pltpu.VMEM((2, rows // 2, norb), BF16),
            pltpu.VMEM((2, rows, norb), BF16),
            pltpu.VMEM((rows, norb), BF16),
            pltpu.VMEM(out, BF16),
            pltpu.SemaphoreType.DMA((COPIES,)),
            pltpu.SemaphoreType.DMA((COPIES,)),
            pltpu.SemaphoreType.DMA((4,)),
            pltpu.SemaphoreType.DMA((8,)),
            pltpu.SemaphoreType.DMA((8,)),
            *[pltpu.SemaphoreType.DMA] * 3,
        ],
        compiler_params=pltpu.CompilerParams(
            collective_id=1, has_side_effects=True, vmem_limit_bytes=56 * 1024 * 1024
        ),
    )(own, coulomb, chosen)


def action_kernel(interp, rows, out):
    out[...] = -jnp.dot(interp[...], rows[...], preferred_element_type=F32)


def action(interp, rows):
    count, listed = interp.shape
    norb = rows.shape[1]
    block = count // 4
    return pl.pallas_call(
        action_kernel,
        grid=(4,),
        out_shape=jax.ShapeDtypeStruct((count, norb), F32),
        in_specs=[pl.BlockSpec((block, listed), lambda i: (i, 0)), pl.BlockSpec((listed, norb), lambda i: (0, 0))],
        out_specs=pl.BlockSpec((block, norb), lambda i: (i, 0)),
    )(interp, rows)


def pick(index, rows, count):
    one_hot = (index[:, None] == jnp.arange(count, dtype=jnp.int32)[None, :]).astype(BF16)
    return jnp.dot(one_hot, rows, preferred_element_type=F32).astype(BF16)


def outgoing_chunks(orbitals, box_counts, owner_map, grid_rows, listed, my_box, box_total, lanes):
    per_owner = LIST // box_total
    box_ids = jnp.arange(box_total, dtype=jnp.int32)
    first_point = jnp.sum(jnp.where(box_ids < my_box, box_counts, 0))
    my_count = jnp.sum(jnp.where(box_ids == my_box, box_counts, 0))
    slot_ids = jnp.arange(SLOTS, dtype=jnp.int32)
    is_live = slot_ids < my_count
    padded = jnp.concatenate([owner_map, jnp.zeros((SLOTS,), jnp.int32)])
    position = lax.dynamic_slice(padded, (first_point,), (SLOTS,))
    owner_ids = position // OWN
    local_ids = position - owner_ids * OWN
    matches = (
        (owner_ids[:, None] == owner_ids[None, :])
        & is_live[None, :]
        & (slot_ids[None, :] < slot_ids[:, None])
    )
    pair_rank = jnp.sum(matches.astype(jnp.int32), axis=1)
    target = jnp.where(is_live, owner_ids * lanes + pair_rank, -1)
    dest = jnp.arange(box_total * lanes, dtype=jnp.int32)
    hits = target[None, :] == dest[:, None]
    coded = (grid_rows[0, :SLOTS] + 1) * OWN + local_ids
    found = jnp.sum(jnp.where(hits, coded[None, :], 0), axis=1)
    grid = found // OWN - 1
    local = jnp.where(found > 0, found - (grid + 1) * OWN, -1)
    meta = jnp.stack([listed[0].reshape(box_total, per_owner), local.reshape(box_total, lanes)], axis=1)
    meta = jnp.pad(meta.astype(BF16), ((0, 0), (lanes - 2, 0), (0, NORB - per_owner)))
    return grid, orbitals, meta


def shards(orbitals, coulomb, interp, box_counts, owner_map, grid_rows, listed):
    box_total = lax.axis_size("row") * lax.axis_size("col")
    lanes = LIST // box_total
    my_box = lax.axis_index("row") * lax.axis_size("col") + lax.axis_index("col")
    received = exchange(
        *outgoing_chunks(orbitals, box_counts, owner_map, grid_rows, listed, my_box, box_total, lanes)
    )
    wanted = received[:, lanes - 2, :lanes].astype(jnp.int32).reshape(-1)
    local = received[:, lanes - 1, :lanes].astype(jnp.int32).reshape(-1)
    place = (local[None, :] == jnp.arange(OWN, dtype=jnp.int32)[:, None]).astype(BF16)
    owned_rows = jnp.dot(
        place, received.reshape(box_total * lanes, NORB), preferred_element_type=F32
    ).astype(BF16)
    chosen = (wanted[:, None] == jnp.arange(OWN, dtype=jnp.int32)[None, :]).astype(BF16)
    fetched = project_rows(owned_rows, coulomb, chosen, box_total)
    return action(interp, fetched.reshape(LIST, NORB))


def solution(mesh):
    return jax.shard_map(
        shards,
        mesh=mesh,
        in_specs=(
            P(BOTH, None),
            P("row", "col"),
            P(BOTH, None),
            P(),
            P(),
            P(BOTH, None),
            P(BOTH, None),
        ),
        out_specs=P(BOTH, None),
        check_vma=False,
    )
```
